32 devices in a mesh: offset: 8 (over z, x), seg: 4 (over y, core).
Axes of the slice: x: 2, y: 2, z: 4, core: 2. Of those that a mesh axis runs over, the one named last changes fastest.
Arguments:
- traces: bfloat16 [1024, 32, 4096], P('offset', 'seg'), may hold values from -1000 to 1000, as said below
- partners: int32 [8, 3], P('offset'), may hold values from 0 to 7, as said below
Outputs:
- correlations: bfloat16 [24, 128, 128, 129], P('offset', 'seg')
The draws below stay inside these ranges and needn't reach their ends.
Inputs may be any that keep to these rules, and one draw needn't show every extreme that they name: `traces`: samples of order one to some hundreds; channels and segments differ in level. `partners`: row a holds 3 distinct blocks, each at most 3 blocks from a (a itself may occur); its first entry lies exactly 3 blocks away.
All inputs are finite; a program needn't handle non-finite values.
Results may differ from the reference program's by a relative error of at most 0.0054.
Values may be sent and summed in bfloat16 or wider, within the bound.
A program may use at most 64 MiB of HBM per device.

```python
import math
import jax
import jax.numpy as jnp
from jax import lax

CH = 128
BINS = 64
SEG_LEN = 4096
FIRST_BIN = 17
HALF_LAG = 64
REACH = 3
PAIR_DEV = 3
BLOCKS = 8
SEGS = 32


def draw_traces(key, part):
    keys = jax.random.split(key, 12)
    channels = BLOCKS * CH
    shape = (channels, SEGS, SEG_LEN)
    noise = jnp.clip(jax.random.normal(keys[0], shape, jnp.float32), -6.0, 6.0)
    growth = 3.0
    chan_gain = jnp.exp(jax.random.uniform(keys[2], (channels, 1, 1), jnp.float32, 0.0, math.log(10.0)))
    position = jnp.arange(SEGS, dtype=jnp.float32) / max(SEGS - 1, 1)
    seg_gain = (growth ** position)[None, :, None] * jax.random.uniform(keys[3], (1, SEGS, 1), jnp.float32, 0.7, 1.4)
    field = noise * chan_gain * seg_gain
    samples = jnp.arange(SEG_LEN, dtype=jnp.float32)[None, None, :]
    for tone in range(4):
        tone_keys = jax.random.split(keys[4 + tone], 3)
        cycles = jax.random.uniform(tone_keys[0], (), jnp.float32, FIRST_BIN, FIRST_BIN + BINS) / SEG_LEN
        amplitude = jnp.exp(jax.random.uniform(tone_keys[1], (channels, 1, 1), jnp.float32, math.log(0.5), math.log(5.0)))
        start_phase = jax.random.uniform(tone_keys[2], (channels, SEGS, 1), jnp.float32, 0.0, 2.0 * math.pi)
        field = field + amplitude * jnp.cos(2.0 * math.pi * cycles * samples + start_phase)
    return field.astype(jnp.bfloat16)


def draw_partners(key, part):
    width = 2 * REACH + 1
    offsets = jnp.arange(width, dtype=jnp.int32) - REACH
    blocks = jnp.arange(BLOCKS, dtype=jnp.int32)
    candidate = blocks[:, None] + offsets[None, :]
    first = jnp.where(blocks + REACH < BLOCKS, blocks + REACH, blocks - REACH)
    valid = (candidate >= 0) & (candidate < BLOCKS) & (candidate != first[:, None])
    score = jax.random.randint(key, (BLOCKS, width), 0, 1 << 20, jnp.int32) * width + jnp.arange(width, dtype=jnp.int32)[None, :]
    score = jnp.where(valid, score, -1 - jnp.arange(width, dtype=jnp.int32)[None, :])
    chosen = lax.top_k(score, PAIR_DEV - 1)[1]
    others = jnp.take_along_axis(candidate, chosen, axis=1)
    return jnp.concatenate([first[:, None], others], axis=1).astype(jnp.int32)


def setup_inputs(seed: int = 0) -> dict:
    streams_of = jax.random.split(jax.random.key(seed), 3)
    return {
        "traces": draw_traces(jax.random.fold_in(streams_of[2], 71), 0),
        "partners": draw_partners(jax.random.fold_in(streams_of[2], 71), 0),
    }


def make_tables(seg_count):
    samples = jnp.arange(SEG_LEN, dtype=jnp.int32)
    bin_index = FIRST_BIN + jnp.arange(BINS, dtype=jnp.int32)
    taper = 0.5 - 0.5 * jnp.cos(2.0 * math.pi * samples.astype(jnp.float32) / SEG_LEN)
    phase = (samples[:, None] * bin_index[None, :] % SEG_LEN).astype(jnp.float32) * (2.0 * math.pi / SEG_LEN)
    forward = jnp.stack([taper[:, None] * jnp.cos(phase), -taper[:, None] * jnp.sin(phase)], axis=-1)
    forward = forward.reshape(SEG_LEN, 2 * BINS).astype(jnp.bfloat16)
    lag_index = jnp.arange(2 * HALF_LAG + 1, dtype=jnp.int32) - HALF_LAG
    turn = (bin_index[:, None] * lag_index[None, :] % SEG_LEN).astype(jnp.float32) * (2.0 * math.pi / SEG_LEN)
    norm_scale = 1.0 / jnp.sqrt(jnp.float32(seg_count * BINS))
    inverse = jnp.stack([jnp.cos(turn), -jnp.sin(turn)], axis=1) * norm_scale
    inverse = inverse.reshape(2 * BINS, 2 * HALF_LAG + 1).astype(jnp.bfloat16)
    return (forward, inverse)

def cross_spectra(first, second):
    first = first.astype(jnp.float32)
    second = second.astype(jnp.float32)
    real_part = jnp.einsum('isk,jsk->ijk', first[..., 0], second[..., 0]) + jnp.einsum('isk,jsk->ijk', first[..., 1], second[..., 1])
    imag_part = jnp.einsum('isk,jsk->ijk', first[..., 1], second[..., 0]) - jnp.einsum('isk,jsk->ijk', first[..., 0], second[..., 1])
    both = jnp.stack([real_part, imag_part], axis=-1)
    return both.reshape(first.shape[0], second.shape[0], -1).astype(jnp.bfloat16)

def reference(traces, partners):
    forward, inverse = make_tables(SEGS)
    blocked = traces.reshape(BLOCKS, CH * SEGS, SEG_LEN)
    spectra = lax.map(lambda block: jnp.dot(block, forward, preferred_element_type=jnp.float32), blocked)
    spectra = spectra.reshape(BLOCKS * CH, SEGS, BINS, 2)
    bin_power = lax.optimization_barrier(jnp.sum(spectra * spectra, axis=(1, 3))) / SEGS
    whitened = (spectra * lax.rsqrt(bin_power + 1e-06)[:, None, :, None]).astype(jnp.bfloat16)
    whitened = whitened.reshape(BLOCKS, CH, SEGS, BINS, 2)
    first_ids = jnp.repeat(jnp.arange(BLOCKS, dtype=jnp.int32), PAIR_DEV)
    second_ids = partners.reshape(-1).astype(jnp.int32)

    def one_pair(ids):
        cross = cross_spectra(whitened[ids[0]], whitened[ids[1]])
        result = jnp.dot(cross.reshape(CH * CH, 2 * BINS), inverse, preferred_element_type=jnp.float32)
        return result.reshape(CH, CH, 2 * HALF_LAG + 1).astype(jnp.bfloat16)
    return lax.map(one_pair, jnp.stack([first_ids, second_ids], axis=1))
```

```python
import functools
import math

import jax
import jax.numpy as jnp
import numpy as np
from jax import lax
from jax.experimental import pallas as pl
from jax.experimental.pallas import tpu as pltpu
from jax.sharding import PartitionSpec as P

BINS = 64
FIRST_BIN = 17
HALF_LAG = 64
REACH = 3
PAIR_DEV = 3
CORES = 2
MESH = pl.DeviceIdType.MESH


def make_tables(seg_count, seg_len):
    samples = np.arange(seg_len, dtype=np.int64)
    bin_index = FIRST_BIN + np.arange(BINS, dtype=np.int64)
    taper = 0.5 - 0.5 * np.cos(2.0 * math.pi * samples / seg_len)
    phase = (samples[:, None] * bin_index[None, :] % seg_len) * (2.0 * math.pi / seg_len)
    forward = np.concatenate(
        [taper[:, None] * np.cos(phase), -taper[:, None] * np.sin(phase)], axis=1
    )
    lag_index = np.arange(2 * HALF_LAG + 1, dtype=np.int64) - HALF_LAG
    turn = (bin_index[:, None] * lag_index[None, :] % seg_len) * (2.0 * math.pi / seg_len)
    scale = 1.0 / math.sqrt(seg_count * BINS)
    inverse = np.concatenate([np.cos(turn), -np.sin(turn)], axis=0) * scale
    return forward.astype(np.float32).astype(jnp.bfloat16), inverse.astype(np.float32).astype(jnp.bfloat16)


def spectra_kernel(seg_local, traces_ref, table_ref, out_ref, flat, turned):
    step = pl.program_id(0)
    rows = traces_ref.shape[0]
    entries = table_ref.shape[1]
    flat[pl.ds(pl.multiple_of(step * rows, rows), rows), :] = jnp.dot(
        traces_ref[...], table_ref[...], preferred_element_type=jnp.float32
    )

    @pl.when(step == pl.num_programs(0) - 1)
    def _():
        channels = flat.shape[0] // seg_local
        for seg in range(seg_local):
            one = flat[pl.ds(seg, channels, stride=seg_local), :]
            turned[pl.ds(seg, entries, stride=seg_local), :] = one.T
        out_ref[...] = turned[...].astype(out_ref.dtype)


def spectra_of(traces, forward):
    channels, seg_local, seg_len = traces.shape
    rows = channels * seg_local
    entries = forward.shape[1]
    tile = 128
    return pl.pallas_call(
        functools.partial(spectra_kernel, seg_local),
        grid=(rows // tile,),
        in_specs=[
            pl.BlockSpec((tile, seg_len), lambda i: (i, 0)),
            pl.BlockSpec((seg_len, entries), lambda i: (0, 0)),
        ],
        out_specs=pl.BlockSpec((entries * seg_local, channels), lambda i: (0, 0)),
        out_shape=jax.ShapeDtypeStruct((entries * seg_local, channels), jnp.bfloat16),
        scratch_shapes=[
            pltpu.VMEM((rows, entries), jnp.float32),
            pltpu.VMEM((entries * seg_local, channels), jnp.float32),
        ],
    )(traces.reshape(rows, seg_len), forward)


def gather_kernel(blocks, segs, own_ref, out_ref, send_sem, recv_sem, mate_sem, local_sem):
    groups = segs // CORES
    block = lax.axis_index("offset")
    seg = lax.axis_index("seg")
    group, core = seg // CORES, seg % CORES
    toward = 2 * (block % 2) - 1
    others = list(range(1, groups))

    def exists(u):
        return jnp.logical_and(block + u * toward >= 0, block + u * toward < blocks)

    def seg_of(g, which):
        return (group + g) % groups * CORES + which

    def slot(u, g, which):
        return out_ref.at[REACH + u * toward, seg_of(g, which)]

    sent = []

    def send(u, g, to_block, to_seg, sem, guard):
        number = len(sent)

        def make():
            return pltpu.make_async_remote_copy(
                src_ref=own_ref if (u, g) == (0, 0) else slot(u, g, core),
                dst_ref=out_ref.at[REACH + block + u * toward - to_block, seg_of(g, core)],
                send_sem=send_sem.at[number],
                recv_sem=sem,
                device_id=(to_block, to_seg),
                device_id_type=MESH,
            )

        sent.append((guard, make))
        when(guard, lambda: make().start())

    def when(guard, do):
        if guard is None:
            do()
        else:
            pl.when(guard)(do)

    def both(*guards):
        kept = [guard for guard in guards if guard is not None]
        return functools.reduce(jnp.logical_and, kept) if kept else None

    def here(u):
        return None if u in (0, -1) else exists(u)

    def back(u, g, at):
        send(u, g, block - 2 * toward, seg, recv_sem.at[at + REACH, g], both(exists(-2), here(u)))

    def ahead(u, g, at):
        send(u, g, block + 2 * toward, seg, recv_sem.at[at + REACH, g], both(exists(2), here(u)))

    def beside(u, g, at):
        send(u, g, block - toward, seg, recv_sem.at[at + REACH, g], here(u))

    def across(u):
        for g in others:
            to_seg = (group - g + groups) % groups * CORES + core
            send(u, 0, block, to_seg, recv_sem.at[u + REACH, g], here(u))

    def swap(u, g):
        send(u, g, block, group * CORES + 1 - core, mate_sem.at[u + REACH, g], here(u))

    def arrived(u, g):
        def wait():
            pltpu.make_async_copy(
                slot(u, g, core), slot(u, g, core), recv_sem.at[u + REACH, g]
            ).wait()

        when(here(u), wait)
        swap(u, g)

    barrier = pltpu.get_barrier_semaphore()

    def greet(to_block, to_seg):
        pl.semaphore_signal(barrier, inc=1, device_id=(to_block, to_seg), device_id_type=MESH)

    greet(block, group * CORES + 1 - core)
    greet(block - toward, seg)
    for g in others:
        greet(block, seg_of(g, core))
    for u in (-2, 2):

        @pl.when(exists(u))
        def _():
            greet(block + u * toward, seg)

    ends = exists(-2).astype(jnp.int32) + exists(2).astype(jnp.int32)
    pl.semaphore_wait(barrier, 2 + len(others) + ends)

    back(0, 0, 2)
    ahead(0, 0, -2)
    beside(0, 0, -1)
    across(0)
    swap(0, 0)
    keep = pltpu.make_async_copy(own_ref, slot(0, 0, core), local_sem)
    keep.start()

    arrived(-1, 0)
    back(-1, 0, 1)
    ahead(-1, 0, -3)
    across(-1)
    for g in others:
        arrived(0, g)
        ahead(0, g, -2)
    arrived(2, 0)
    arrived(-2, 0)
    arrived(1, 0)
    back(1, 0, 3)
    for g in others:
        back(0, g, 2)
    for g in others:
        arrived(-1, g)
        ahead(-1, g, -3)
    arrived(-3, 0)
    arrived(3, 0)
    across(3)
    for g in others:
        arrived(-2, g)
        beside(-2, g, 1)
    for u in (2, -3, 1, 3):
        for g in others:
            arrived(u, g)

    keep.wait()
    for u in range(-REACH, REACH + 1):
        for g in range(groups):

            def wait(u=u, g=g):
                pltpu.make_async_copy(
                    slot(u, g, 1 - core), slot(u, g, 1 - core), mate_sem.at[u + REACH, g]
                ).wait()

            when(here(u), wait)
    for guard, make in sent:
        when(guard, lambda make=make: make().wait_send())


def gathered(chunk, blocks, segs):
    groups = segs // CORES
    sends = (5 + 2 * REACH + 1) * groups + 8 * groups + 8
    width = 2 * REACH + 1
    return pl.pallas_call(
        functools.partial(gather_kernel, blocks, segs),
        out_shape=jax.ShapeDtypeStruct((width, segs) + chunk.shape, chunk.dtype),
        in_specs=[pl.BlockSpec(memory_space=pltpu.VMEM)],
        out_specs=pl.BlockSpec(memory_space=pl.ANY),
        scratch_shapes=[
            pltpu.SemaphoreType.DMA((sends,)),
            pltpu.SemaphoreType.DMA((width, groups)),
            pltpu.SemaphoreType.DMA((width, groups)),
            pltpu.SemaphoreType.DMA,
        ],
        compiler_params=pltpu.CompilerParams(collective_id=0, has_side_effects=True),
    )(chunk)


def cross_kernel(seg_total, place_ref, own_ref, *rest):
    other_refs, out_ref = rest[:-1], rest[-1]
    bins = own_ref.shape[1]
    half = own_ref.shape[3] // 2

    for k in range(bins):
        parts = []
        for ref in other_refs:
            block = ref[0, :, :, k].astype(jnp.float32)
            block = block.reshape(-1, block.shape[-1])
            power = jnp.sum(block * block, axis=0, keepdims=True) / seg_total
            parts.append((block * lax.rsqrt(power + 1e-06)).astype(jnp.bfloat16))
        other = jnp.concatenate(parts, axis=1)
        product = lax.dot_general(
            own_ref[0, k], other, (((0,), (0,)), ((), ())), preferred_element_type=jnp.float32
        ).astype(out_ref.dtype)
        channels = parts[0].shape[1]
        for pair in range(len(parts)):
            piece = product[:, pair * channels : (pair + 1) * channels]
            out_ref[0, k, pair] = piece[:half]
            out_ref[1, k, pair] = piece[half:]


def cross_of(places, own, around, rows, seg_total):
    width, segs, _, bins, seg_local, channels = around.shape
    tile = 8

    def other(pair):
        return pl.BlockSpec(
            (1, segs, 2, tile, seg_local, channels),
            lambda i, place, pair=pair: (place[pair], 0, 0, i, 0, 0),
        )

    depth, columns = own.shape[2:]
    return pl.pallas_call(
        functools.partial(cross_kernel, seg_total),
        grid_spec=pltpu.PrefetchScalarGridSpec(
            num_scalar_prefetch=1,
            grid=(bins // tile,),
            in_specs=[pl.BlockSpec((1, tile, depth, columns), lambda i, place: (0, i, 0, 0))]
            + [other(pair) for pair in range(PAIR_DEV)],
            out_specs=pl.BlockSpec(
                (2, tile, PAIR_DEV, rows, channels), lambda i, place: (0, i, 0, 0, 0)
            ),
        ),
        out_shape=jax.ShapeDtypeStruct((2, bins, PAIR_DEV, rows, channels), jnp.bfloat16),
    )(places, own, *([around] * PAIR_DEV))


def per_device(traces, partners):
    channels, seg_local, seg_len = traces.shape
    segs = lax.axis_size("seg")
    blocks = lax.axis_size("offset")
    seg_total = seg_local * segs
    rows = channels // segs
    forward, inverse = make_tables(seg_total, seg_len)
    chunk = spectra_of(traces, jnp.asarray(forward))
    around = gathered(chunk, blocks, segs)
    around = around.reshape(2 * REACH + 1, segs, 2, BINS, seg_local, channels)
    own = lax.dynamic_slice_in_dim(around[REACH], lax.axis_index("seg") * rows, rows, axis=4)
    own = own.astype(jnp.float32)
    power = jnp.sum(own * own, axis=(0, 1, 3)) / seg_total
    own = own * lax.rsqrt(power + 1e-06)[None, None, :, None, :]
    real, imag = own[:, 0], own[:, 1]
    left = jnp.stack([jnp.stack([real, imag], axis=1), jnp.stack([imag, -real], axis=1)], axis=4)
    left = left.transpose(2, 0, 1, 3, 4, 5).reshape(1, BINS, segs * 2 * seg_local, 2 * rows)
    places = partners[0] + REACH - lax.axis_index("offset")
    cross = cross_of(places, left.astype(jnp.bfloat16), around, rows, seg_total)
    cross = cross.reshape(2 * BINS, PAIR_DEV, rows, channels)
    result = jnp.einsum(
        "epij,el->pijl", cross, jnp.asarray(inverse), preferred_element_type=jnp.float32
    )
    return result.astype(jnp.bfloat16)


def solution(mesh):
    in_specs = (P("offset", "seg", None), P("offset", None))
    out_specs = P("offset", "seg", None, None)
    return jax.shard_map(
        per_device, mesh=mesh, in_specs=in_specs, out_specs=out_specs, check_vma=False
    )
```

```python
import functools
import math

import jax
import jax.numpy as jnp
import numpy as np
from jax import lax
from jax.experimental import pallas as pl
from jax.experimental.pallas import tpu as pltpu
from jax.sharding import PartitionSpec as P

BINS = 64
FIRST_BIN = 17
HALF_LAG = 64
REACH = 3
PAIR_DEV = 3
CORES = 2
HALVES = 2
MESH = pl.DeviceIdType.MESH


def make_tables(seg_count, seg_len):
    samples = np.arange(seg_len, dtype=np.int64)
    bin_index = FIRST_BIN + np.arange(BINS, dtype=np.int64)
    taper = 0.5 - 0.5 * np.cos(2.0 * math.pi * samples / seg_len)
    phase = (samples[:, None] * bin_index[None, :] % seg_len) * (2.0 * math.pi / seg_len)
    forward = np.concatenate(
        [taper[:, None] * np.cos(phase), -taper[:, None] * np.sin(phase)], axis=1
    )
    lag_index = np.arange(2 * HALF_LAG + 1, dtype=np.int64) - HALF_LAG
    turn = (bin_index[:, None] * lag_index[None, :] % seg_len) * (2.0 * math.pi / seg_len)
    scale = 1.0 / math.sqrt(seg_count * BINS)
    inverse = np.concatenate([np.cos(turn), -np.sin(turn)], axis=0) * scale
    return forward.astype(np.float32).astype(jnp.bfloat16), inverse.astype(np.float32).astype(jnp.bfloat16)


def spectra_kernel(seg_local, traces_ref, table_ref, out_ref, flat, turned):
    step = pl.program_id(0)
    entries = table_ref.shape[1]
    part = jnp.dot(traces_ref[...], table_ref[...], preferred_element_type=jnp.float32)

    @pl.when(step == 0)
    def _():
        flat[...] = part

    @pl.when(step > 0)
    def _():
        flat[...] += part

    @pl.when(step == pl.num_programs(0) - 1)
    def _():
        channels = flat.shape[0] // seg_local
        for seg in range(seg_local):
            one = flat[pl.ds(seg, channels, stride=seg_local), :]
            turned[pl.ds(seg, entries, stride=seg_local), :] = one.T
        out_ref[...] = turned[...].astype(out_ref.dtype)


def spectra_of(traces, forward):
    channels, seg_local, seg_len = traces.shape
    rows = channels * seg_local
    entries = forward.shape[1]
    tile = 512
    return pl.pallas_call(
        functools.partial(spectra_kernel, seg_local),
        grid=(seg_len // tile,),
        in_specs=[
            pl.BlockSpec((rows, tile), lambda i: (0, i)),
            pl.BlockSpec((tile, entries), lambda i: (i, 0)),
        ],
        out_specs=pl.BlockSpec((entries * seg_local, channels), lambda i: (0, 0)),
        out_shape=jax.ShapeDtypeStruct((entries * seg_local, channels), jnp.bfloat16),
        scratch_shapes=[
            pltpu.VMEM((rows, entries), jnp.float32),
            pltpu.VMEM((entries * seg_local, channels), jnp.float32),
        ],
    )(traces.reshape(rows, seg_len), forward)


def gather_kernel(blocks, segs, own_ref, out_ref, send_sem, recv_sem, mate_sem, local_sem):
    groups = segs // CORES
    block = lax.axis_index("offset")
    seg = lax.axis_index("seg")
    group, core = seg // CORES, seg % CORES
    toward = 2 * (block % 2) - 1
    others = list(range(1, groups))

    def exists(u):
        return jnp.logical_and(block + u * toward >= 0, block + u * toward < blocks)

    def seg_of(g, which):
        return (group + g) % groups * CORES + which

    half = own_ref.shape[0] // HALVES

    def part(h):
        return pl.ds(h * half, half)

    def slot(u, g, h, which):
        return out_ref.at[REACH + u * toward, seg_of(g, which), part(h)]

    sent = []

    def when(guard, do):
        if guard is None:
            do()
        else:
            pl.when(guard)(do)

    def both(*guards):
        kept = [guard for guard in guards if guard is not None]
        return functools.reduce(jnp.logical_and, kept) if kept else None

    def here(u):
        return None if u in (0, -1) else exists(u)

    def send(u, g, h, to_block, to_seg, sem, guard):
        number = len(sent)

        def make():
            return pltpu.make_async_remote_copy(
                src_ref=own_ref.at[part(h)] if (u, g) == (0, 0) else slot(u, g, h, core),
                dst_ref=out_ref.at[
                    REACH + block + u * toward - to_block, seg_of(g, core), part(h)
                ],
                send_sem=send_sem.at[number],
                recv_sem=sem,
                device_id=(to_block, to_seg),
                device_id_type=MESH,
            )

        sent.append((guard, make))
        when(guard, lambda: make().start())

    def back(u, g, h):
        at = recv_sem.at[u + 2 + REACH, g, h]
        send(u, g, h, block - 2 * toward, seg, at, both(exists(-2), here(u)))

    def ahead(u, g, h):
        at = recv_sem.at[u - 2 + REACH, g, h]
        send(u, g, h, block + 2 * toward, seg, at, both(exists(2), here(u)))

    def beside(u, g, h):
        at = recv_sem.at[-1 - u + REACH, g, h]
        send(u, g, h, block - toward, seg, at, here(u))

    def across(u, h):
        for g in others:
            to_seg = (group - g + groups) % groups * CORES + core
            send(u, 0, h, block, to_seg, recv_sem.at[u + REACH, g, h], here(u))

    def swap(u, g, h):
        at = mate_sem.at[u + REACH, g, h]
        send(u, g, h, block, group * CORES + 1 - core, at, here(u))

    def arrived(u, g, h):
        def wait():
            here_now = slot(u, g, h, core)
            pltpu.make_async_copy(here_now, here_now, recv_sem.at[u + REACH, g, h]).wait()

        when(here(u), wait)
        swap(u, g, h)

    barrier = pltpu.get_barrier_semaphore()

    def greet(to_block, to_seg):
        pl.semaphore_signal(barrier, inc=1, device_id=(to_block, to_seg), device_id_type=MESH)

    greet(block, group * CORES + 1 - core)
    greet(block - toward, seg)
    for g in others:
        greet(block, seg_of(g, core))
    for u in (-2, 2):

        @pl.when(exists(u))
        def _():
            greet(block + u * toward, seg)

    ends = exists(-2).astype(jnp.int32) + exists(2).astype(jnp.int32)
    pl.semaphore_wait(barrier, 2 + len(others) + ends)

    every = range(HALVES)
    for h in every:
        across(0, h)
        beside(0, 0, h)
        back(0, 0, h)
        ahead(0, 0, h)
    for h in every:
        swap(0, 0, h)
    whole = out_ref.at[REACH, seg]
    keep = pltpu.make_async_copy(own_ref, whole, local_sem)
    keep.start()

    for h in every:
        arrived(-1, 0, h)
        back(-1, 0, h)
        ahead(-1, 0, h)
        for g in others:
            arrived(0, g, h)
            beside(0, g, h)
        arrived(2, 0, h)
        if h >= HALVES // 2:
            across(2, h)
        arrived(-2, 0, h)
    for g in others:
        for h in every:
            ahead(0, g, h)
    for h in every:
        arrived(1, 0, h)
        back(1, 0, h)
        arrived(-3, 0, h)
        if h >= HALVES // 2:
            across(-3, h)
    for g in others:
        for h in range(HALVES // 2):
            back(0, g, h)
    for h in every:
        for g in others:
            arrived(-1, g, h)
            if h < HALVES // 2:
                ahead(-1, g, h)
    for g in others:
        for h in range(HALVES // 2, HALVES):
            arrived(2, g, h)
    for h in every:
        arrived(3, 0, h)
        across(3, h)
        for g in others:
            arrived(-2, g, h)
            beside(-2, g, h)
    for g in others:
        for h in range(HALVES // 2, HALVES):
            arrived(-3, g, h)
        for h in range(HALVES // 2):
            arrived(2, g, h)
            arrived(-3, g, h)
        for h in every:
            arrived(1, g, h)
            arrived(3, g, h)

    keep.wait()
    for u in range(-REACH, REACH + 1):
        for g in range(groups):
            for h in every:

                def wait(u=u, g=g, h=h):
                    theirs = slot(u, g, h, 1 - core)
                    pltpu.make_async_copy(
                        theirs, theirs, mate_sem.at[u + REACH, g, h]
                    ).wait()

                when(here(u), wait)
    for guard, make in sent:
        when(guard, lambda make=make: make().wait_send())


def gathered(chunk, blocks, segs):
    groups = segs // CORES
    sends = (16 * groups + 8) * HALVES
    width = 2 * REACH + 1
    return pl.pallas_call(
        functools.partial(gather_kernel, blocks, segs),
        out_shape=jax.ShapeDtypeStruct((width, segs) + chunk.shape, chunk.dtype),
        in_specs=[pl.BlockSpec(memory_space=pltpu.VMEM)],
        out_specs=pl.BlockSpec(memory_space=pl.ANY),
        scratch_shapes=[
            pltpu.SemaphoreType.DMA((sends,)),
            pltpu.SemaphoreType.DMA((width, groups, HALVES)),
            pltpu.SemaphoreType.DMA((width, groups, HALVES)),
            pltpu.SemaphoreType.DMA,
        ],
        compiler_params=pltpu.CompilerParams(collective_id=0, has_side_effects=True),
    )(chunk)


def whitened(ref, k, seg_total):
    block = ref[0, :, :, k].astype(jnp.float32)
    block = block.reshape(-1, block.shape[-1])
    power = jnp.sum(block * block, axis=0, keepdims=True) / seg_total
    return block * lax.rsqrt(power + 1e-06)


def cross_kernel(seg_total, rows, partners_ref, own_ref, *rest):
    other_refs, out_ref = rest[:-1], rest[-1]
    segs, _, bins, seg_local, channels = own_ref.shape[1:]
    shift = (channels - lax.axis_index("seg") * rows) % channels
    lane = lax.broadcasted_iota(jnp.int32, (segs * 2 * seg_local, channels), 1)

    for k in range(bins):
        own = pltpu.roll(whitened(own_ref, k, seg_total), shift, 1)
        split = own.reshape(segs, 2, seg_local, channels)
        turned = jnp.stack([split[:, 1], -split[:, 0]], axis=1).reshape(own.shape)
        own = jnp.where(lane < rows, own, pltpu.roll(turned, rows, 1))
        own = own[:, : 2 * rows].astype(jnp.bfloat16)
        parts = [whitened(ref, k, seg_total).astype(jnp.bfloat16) for ref in other_refs]
        product = lax.dot_general(
            own,
            jnp.concatenate(parts, axis=1),
            (((0,), (0,)), ((), ())),
            preferred_element_type=jnp.float32,
        ).astype(out_ref.dtype)
        for pair in range(len(parts)):
            piece = product[:, pair * channels : (pair + 1) * channels]
            out_ref[0, k, pair] = piece[:rows]
            out_ref[1, k, pair] = piece[rows:]


def cross_of(partners, around, rows, seg_total):
    width, segs, _, bins, seg_local, channels = around.shape
    tile = 16

    def part_of(place):
        return pl.BlockSpec(
            (1, segs, 2, tile, seg_local, channels),
            lambda i, partners: (place(partners), 0, 0, i, 0, 0),
        )

    def other(pair):
        return part_of(lambda partners: partners[0, pair] + REACH - lax.axis_index("offset"))

    return pl.pallas_call(
        functools.partial(cross_kernel, seg_total, rows),
        grid_spec=pltpu.PrefetchScalarGridSpec(
            num_scalar_prefetch=1,
            grid=(bins // tile,),
            in_specs=[part_of(lambda partners: REACH)]
            + [other(pair) for pair in range(PAIR_DEV)],
            out_specs=pl.BlockSpec(
                (2, tile, PAIR_DEV, rows, channels), lambda i, partners: (0, i, 0, 0, 0)
            ),
        ),
        out_shape=jax.ShapeDtypeStruct((2, bins, PAIR_DEV, rows, channels), jnp.bfloat16),
    )(partners, *([around] * (1 + PAIR_DEV)))


def per_device(traces, partners):
    channels, seg_local, seg_len = traces.shape
    segs = lax.axis_size("seg")
    blocks = lax.axis_size("offset")
    seg_total = seg_local * segs
    rows = channels // segs
    forward, inverse = make_tables(seg_total, seg_len)
    chunk = spectra_of(traces, jnp.asarray(forward))
    around = gathered(chunk, blocks, segs)
    around = around.reshape(2 * REACH + 1, segs, 2, BINS, seg_local, channels)
    cross = cross_of(partners, around, rows, seg_total)
    cross = cross.reshape(2 * BINS, PAIR_DEV, rows, channels)
    result = jnp.einsum(
        "epij,el->pijl", cross, jnp.asarray(inverse), preferred_element_type=jnp.float32
    )
    return result.astype(jnp.bfloat16)


def solution(mesh):
    in_specs = (P("offset", "seg", None), P("offset", None))
    out_specs = P("offset", "seg", None, None)
    return jax.shard_map(
        per_device, mesh=mesh, in_specs=in_specs, out_specs=out_specs, check_vma=False
    )
```

```python
import functools
import math

import jax
import jax.numpy as jnp
import numpy as np
from jax import lax
from jax.experimental import pallas as pl
from jax.experimental.pallas import tpu as pltpu
from jax.sharding import PartitionSpec as P

BINS = 64
FIRST_BIN = 17
HALF_LAG = 64
REACH = 3
PAIR_DEV = 3
CORES = 2
HALVES = 2
MESH = pl.DeviceIdType.MESH


def make_tables(seg_count, seg_len):
    samples = np.arange(seg_len, dtype=np.int64)
    bin_index = FIRST_BIN + np.arange(BINS, dtype=np.int64)
    taper = 0.5 - 0.5 * np.cos(2.0 * math.pi * samples / seg_len)
    phase = (samples[:, None] * bin_index[None, :] % seg_len) * (2.0 * math.pi / seg_len)
    forward = np.concatenate(
        [taper[:, None] * np.cos(phase), -taper[:, None] * np.sin(phase)], axis=1
    )
    lag_index = np.arange(2 * HALF_LAG + 1, dtype=np.int64) - HALF_LAG
    turn = (bin_index[:, None] * lag_index[None, :] % seg_len) * (2.0 * math.pi / seg_len)
    scale = 1.0 / math.sqrt(seg_count * BINS)
    inverse = np.concatenate([np.cos(turn), -np.sin(turn)], axis=0) * scale
    return forward.astype(np.float32).astype(jnp.bfloat16), inverse.astype(np.float32).astype(jnp.bfloat16)


def spectra_kernel(seg_local, traces_ref, table_ref, out_ref, flat, turned):
    step = pl.program_id(0)
    rows = traces_ref.shape[0]
    entries = table_ref.shape[1]
    flat[pl.ds(pl.multiple_of(step * rows, rows), rows), :] = jnp.dot(
        traces_ref[...], table_ref[...], preferred_element_type=jnp.float32
    )

    @pl.when(step == pl.num_programs(0) - 1)
    def _():
        channels = flat.shape[0] // seg_local
        for seg in range(seg_local):
            one = flat[pl.ds(seg, channels, stride=seg_local), :]
            turned[pl.ds(seg, entries, stride=seg_local), :] = one.T
        out_ref[...] = turned[...].astype(out_ref.dtype)


def spectra_of(traces, forward):
    channels, seg_local, seg_len = traces.shape
    rows = channels * seg_local
    entries = forward.shape[1]
    tile = 512
    return pl.pallas_call(
        functools.partial(spectra_kernel, seg_local),
        grid=(rows // tile,),
        in_specs=[
            pl.BlockSpec((tile, seg_len), lambda i: (i, 0)),
            pl.BlockSpec((seg_len, entries), lambda i: (0, 0)),
        ],
        out_specs=pl.BlockSpec((entries * seg_local, channels), lambda i: (0, 0)),
        out_shape=jax.ShapeDtypeStruct((entries * seg_local, channels), jnp.bfloat16),
        scratch_shapes=[
            pltpu.VMEM((rows, entries), jnp.float32),
            pltpu.VMEM((entries * seg_local, channels), jnp.float32),
        ],
    )(traces.reshape(rows, seg_len), forward)


def gather_kernel(blocks, segs, own_ref, out_ref, send_sem, recv_sem, mate_sem, local_sem):
    groups = segs // CORES
    block = lax.axis_index("offset")
    seg = lax.axis_index("seg")
    group, core = seg // CORES, seg % CORES
    toward = 2 * (block % 2) - 1
    others = list(range(1, groups))

    def exists(u):
        return jnp.logical_and(block + u * toward >= 0, block + u * toward < blocks)

    def seg_of(g, which):
        return (group + g) % groups * CORES + which

    half = own_ref.shape[0] // HALVES

    def part(h):
        return pl.ds(h * half, half)

    def slot(u, g, h, which):
        return out_ref.at[REACH + u * toward, seg_of(g, which), part(h)]

    sent = []

    def when(guard, do):
        if guard is None:
            do()
        else:
            pl.when(guard)(do)

    def both(*guards):
        kept = [guard for guard in guards if guard is not None]
        return functools.reduce(jnp.logical_and, kept) if kept else None

    def here(u):
        return None if u in (0, -1) else exists(u)

    def send(u, g, h, to_block, to_seg, sem, guard):
        number = len(sent)

        def make():
            return pltpu.make_async_remote_copy(
                src_ref=own_ref.at[part(h)] if (u, g) == (0, 0) else slot(u, g, h, core),
                dst_ref=out_ref.at[
                    REACH + block + u * toward - to_block, seg_of(g, core), part(h)
                ],
                send_sem=send_sem.at[number],
                recv_sem=sem,
                device_id=(to_block, to_seg),
                device_id_type=MESH,
            )

        sent.append((guard, make))
        when(guard, lambda: make().start())

    def back(u, g, h):
        at = recv_sem.at[u + 2 + REACH, g, h]
        send(u, g, h, block - 2 * toward, seg, at, both(exists(-2), here(u)))

    def ahead(u, g, h):
        at = recv_sem.at[u - 2 + REACH, g, h]
        send(u, g, h, block + 2 * toward, seg, at, both(exists(2), here(u)))

    def beside(u, g, h):
        at = recv_sem.at[-1 - u + REACH, g, h]
        send(u, g, h, block - toward, seg, at, here(u))

    def across(u, h):
        for g in others:
            to_seg = (group - g + groups) % groups * CORES + core
            send(u, 0, h, block, to_seg, recv_sem.at[u + REACH, g, h], here(u))

    def swap(u, g, h):
        at = mate_sem.at[u + REACH, g, h]
        send(u, g, h, block, group * CORES + 1 - core, at, here(u))

    def arrived(u, g, h):
        def wait():
            here_now = slot(u, g, h, core)
            pltpu.make_async_copy(here_now, here_now, recv_sem.at[u + REACH, g, h]).wait()

        when(here(u), wait)
        swap(u, g, h)

    barrier = pltpu.get_barrier_semaphore()

    def greet(to_block, to_seg):
        pl.semaphore_signal(barrier, inc=1, device_id=(to_block, to_seg), device_id_type=MESH)

    greet(block, group * CORES + 1 - core)
    greet(block - toward, seg)
    for g in others:
        greet(block, seg_of(g, core))
    for u in (-2, 2):

        @pl.when(exists(u))
        def _():
            greet(block + u * toward, seg)

    ends = exists(-2).astype(jnp.int32) + exists(2).astype(jnp.int32)
    pl.semaphore_wait(barrier, 2 + len(others) + ends)

    every = range(HALVES)
    for h in every:
        across(0, h)
        beside(0, 0, h)
        back(0, 0, h)
        ahead(0, 0, h)
    for h in every:
        swap(0, 0, h)
    whole = out_ref.at[REACH, seg]
    keep = pltpu.make_async_copy(own_ref, whole, local_sem)
    keep.start()

    for h in every:
        arrived(-1, 0, h)
        back(-1, 0, h)
        ahead(-1, 0, h)
        for g in others:
            arrived(0, g, h)
            beside(0, g, h)
        arrived(2, 0, h)
        if h >= HALVES // 2:
            across(2, h)
        arrived(-2, 0, h)
    for g in others:
        for h in every:
            ahead(0, g, h)
    for h in every:
        arrived(1, 0, h)
        back(1, 0, h)
        arrived(-3, 0, h)
        if h >= HALVES // 2:
            across(-3, h)
    for g in others:
        for h in range(HALVES // 2):
            back(0, g, h)
    for h in every:
        for g in others:
            arrived(-1, g, h)
            if h < HALVES // 2:
                ahead(-1, g, h)
    for g in others:
        for h in range(HALVES // 2, HALVES):
            arrived(2, g, h)
    for h in every:
        arrived(3, 0, h)
        across(3, h)
        for g in others:
            arrived(-2, g, h)
            beside(-2, g, h)
    for g in others:
        for h in range(HALVES // 2, HALVES):
            arrived(-3, g, h)
        for h in range(HALVES // 2):
            arrived(2, g, h)
            arrived(-3, g, h)
        for h in every:
            arrived(1, g, h)
            arrived(3, g, h)

    keep.wait()
    for u in range(-REACH, REACH + 1):
        for g in range(groups):
            for h in every:

                def wait(u=u, g=g, h=h):
                    theirs = slot(u, g, h, 1 - core)
                    pltpu.make_async_copy(
                        theirs, theirs, mate_sem.at[u + REACH, g, h]
                    ).wait()

                when(here(u), wait)
    for guard, make in sent:
        when(guard, lambda make=make: make().wait_send())


def gathered(chunk, blocks, segs):
    groups = segs // CORES
    sends = (16 * groups + 8) * HALVES
    width = 2 * REACH + 1
    return pl.pallas_call(
        functools.partial(gather_kernel, blocks, segs),
        out_shape=jax.ShapeDtypeStruct((width, segs) + chunk.shape, chunk.dtype),
        in_specs=[pl.BlockSpec(memory_space=pltpu.VMEM)],
        out_specs=pl.BlockSpec(memory_space=pl.ANY),
        scratch_shapes=[
            pltpu.SemaphoreType.DMA((sends,)),
            pltpu.SemaphoreType.DMA((width, groups, HALVES)),
            pltpu.SemaphoreType.DMA((width, groups, HALVES)),
            pltpu.SemaphoreType.DMA,
        ],
        compiler_params=pltpu.CompilerParams(collective_id=0, has_side_effects=True),
    )(chunk)


def whitened(ref, k, seg_total):
    block = ref[0, :, :, k].astype(jnp.float32)
    block = block.reshape(-1, block.shape[-1])
    power = jnp.sum(block * block, axis=0, keepdims=True) / seg_total
    return block * lax.rsqrt(power + 1e-06)


def cross_kernel(seg_total, rows, partners_ref, own_ref, *rest):
    other_refs, out_ref = rest[:-1], rest[-1]
    segs, _, bins, seg_local, channels = own_ref.shape[1:]
    shift = (channels - lax.axis_index("seg") * rows) % channels
    lane = lax.broadcasted_iota(jnp.int32, (segs * 2 * seg_local, channels), 1)

    for k in range(bins):
        own = pltpu.roll(whitened(own_ref, k, seg_total), shift, 1)
        split = own.reshape(segs, 2, seg_local, channels)
        turned = jnp.stack([split[:, 1], -split[:, 0]], axis=1).reshape(own.shape)
        own = jnp.where(lane < rows, own, pltpu.roll(turned, rows, 1))
        own = own[:, : 2 * rows].astype(jnp.bfloat16)
        parts = [whitened(ref, k, seg_total).astype(jnp.bfloat16) for ref in other_refs]
        product = lax.dot_general(
            own,
            jnp.concatenate(parts, axis=1),
            (((0,), (0,)), ((), ())),
            preferred_element_type=jnp.float32,
        ).astype(out_ref.dtype)
        for pair in range(len(parts)):
            piece = product[:, pair * channels : (pair + 1) * channels]
            out_ref[0, k, pair] = piece[:rows]
            out_ref[1, k, pair] = piece[rows:]


def cross_of(partners, around, rows, seg_total):
    width, segs, _, bins, seg_local, channels = around.shape
    tile = 16

    def part_of(place):
        return pl.BlockSpec(
            (1, segs, 2, tile, seg_local, channels),
            lambda i, partners: (place(partners), 0, 0, i, 0, 0),
        )

    def other(pair):
        return part_of(lambda partners: partners[0, pair] + REACH - lax.axis_index("offset"))

    return pl.pallas_call(
        functools.partial(cross_kernel, seg_total, rows),
        grid_spec=pltpu.PrefetchScalarGridSpec(
            num_scalar_prefetch=1,
            grid=(bins // tile,),
            in_specs=[part_of(lambda partners: REACH)]
            + [other(pair) for pair in range(PAIR_DEV)],
            out_specs=pl.BlockSpec(
                (2, tile, PAIR_DEV, rows, channels), lambda i, partners: (0, i, 0, 0, 0)
            ),
        ),
        out_shape=jax.ShapeDtypeStruct((2, bins, PAIR_DEV, rows, channels), jnp.bfloat16),
    )(partners, *([around] * (1 + PAIR_DEV)))


def per_device(traces, partners):
    channels, seg_local, seg_len = traces.shape
    segs = lax.axis_size("seg")
    blocks = lax.axis_size("offset")
    seg_total = seg_local * segs
    rows = channels // segs
    forward, inverse = make_tables(seg_total, seg_len)
    chunk = spectra_of(traces, jnp.asarray(forward))
    around = gathered(chunk, blocks, segs)
    around = around.reshape(2 * REACH + 1, segs, 2, BINS, seg_local, channels)
    cross = cross_of(partners, around, rows, seg_total)
    cross = cross.reshape(2 * BINS, PAIR_DEV, rows, channels)
    result = jnp.einsum(
        "epij,el->pijl", cross, jnp.asarray(inverse), preferred_element_type=jnp.float32
    )
    return result.astype(jnp.bfloat16)


def solution(mesh):
    in_specs = (P("offset", "seg", None), P("offset", None))
    out_specs = P("offset", "seg", None, None)
    return jax.shard_map(
        per_device, mesh=mesh, in_specs=in_specs, out_specs=out_specs, check_vma=False
    )
```
